768 devices in a mesh: dp: 8 (over x, core), ctx: 96 (over y, z).
Axes of the slice: x: 4, y: 8, z: 12, core: 2. Of those that a mesh axis runs over, the one named last changes fastest.
Arguments:
- queries: bfloat16 [8, 12288, 4096], P('dp', 'ctx'), may hold values from -250 to 250
- keys: bfloat16 [8, 12288, 512], P('dp', 'ctx'), may hold values from -4 to 4
- values: bfloat16 [8, 12288, 512], P('dp', 'ctx'), may hold values from -6 to 6
- logp_grad: bfloat16 [8, 12288, 4096], P('dp', 'ctx'), may hold values from -6 to 6
- response_ids: int32 [8, 12288], P('dp', 'ctx'), may hold values from 0 to 47, as said below
- sample_ids: int32 [8, 48], P('dp'), may hold values from 0 to 47, as said below
- rewards: float32 [8, 48], P('dp'), may hold values from 0 to 1
- new_logp: float32 [8, 12288], P('dp', 'ctx'), may hold values from -4 to 0
- old_logp: float32 [8, 12288], P('dp', 'ctx'), may hold values from -4 to 0
Outputs:
- query_grad: bfloat16 [8, 12288, 4096], P('dp', 'ctx')
- key_grad: bfloat16 [8, 12288, 512], P('dp', 'ctx')
- value_grad: bfloat16 [8, 12288, 512], P('dp', 'ctx')
- token_ratio: float32 [8, 12288], P('dp', 'ctx')
- advantage: float32 [8, 48], P('dp')
The draws below stay inside these ranges and needn't reach their ends.
Inputs may be any that keep to these rules, and one draw needn't show every extreme that they name: `response_ids`: along each packed row the ids never fall; every id names 128 to 384 consecutive positions, and some id names exactly 384. `sample_ids`: each prompt id names exactly 8 responses of the whole batch.
All inputs are finite; a program needn't handle non-finite values.
Results may differ from the reference program's by a relative error of at most 0.015.
Values may be sent and summed in bfloat16 or wider, within the bound.
No kernel may reach another device: no remote copies, remote signals or barrier semaphores. Data moves between devices by JAX's collectives and lax.ppermute only.
A program may use at most 32 MiB of HBM per device.

```python
import math
import jax
import jax.numpy as jnp
from jax import lax

TOK_DEV = 128
QHEADS = 32
KVHEADS = 4
HEAD_DIM = 128
SPAN = 3
GROUP = 8
LENGTH = 12288
PACKS = 8
RESP_PACK = 48
SAMPLES = 48
MEAN_LEN = 256


def paired_fields(seed_key):
    base_key = jax.random.fold_in(seed_key, 11)
    group_heads = QHEADS // KVHEADS
    key_field = jax.random.normal(jax.random.fold_in(base_key, 1), (PACKS, LENGTH, KVHEADS, HEAD_DIM), jnp.float32)
    key_field = jnp.clip(key_field, -4.0, 4.0)
    query_shape = (PACKS, LENGTH, KVHEADS, group_heads, HEAD_DIM)
    query_field = jax.random.normal(jax.random.fold_in(base_key, 2), query_shape, jnp.float32)
    query_field = jnp.clip(query_field, -6.0, 6.0)
    return (query_field.reshape(PACKS, LENGTH, QHEADS * HEAD_DIM), key_field.reshape(PACKS, LENGTH, KVHEADS * HEAD_DIM))


def draw_queries(key, part):
    return paired_fields(key)[0].astype(jnp.bfloat16)


def draw_keys(key, part):
    return paired_fields(key)[1].astype(jnp.bfloat16)


def draw_response_ids(key, part):
    base_key = jax.random.fold_in(key, 23)
    half_count = RESP_PACK // 2
    shifts = jax.random.randint(jax.random.fold_in(base_key, 1), (PACKS, half_count), 0, TOK_DEV + 1)
    widest = jax.random.randint(jax.random.fold_in(base_key, 2), (PACKS, 1), 0, half_count)
    shifts = jnp.where(jnp.arange(half_count)[None, :] == widest, TOK_DEV, shifts)
    span_rows = jnp.concatenate([2 * TOK_DEV + shifts, 2 * TOK_DEV - shifts], axis=1)
    row_keys = jax.random.split(jax.random.fold_in(base_key, 3), PACKS)
    orders = jax.vmap(lambda row_key: jax.random.permutation(row_key, RESP_PACK))(row_keys)
    span_rows = jnp.take_along_axis(span_rows, orders, axis=1)
    end_points = jnp.cumsum(span_rows, axis=1)
    positions = jnp.arange(LENGTH)
    passed = (end_points[:, None, :] <= positions[None, :, None]).astype(jnp.int32)
    return jnp.sum(passed, axis=2).astype(jnp.int32)


def draw_sample_ids(key, part):
    shuffled = jax.random.permutation(jax.random.fold_in(key, 31), PACKS * RESP_PACK)
    return (shuffled % SAMPLES).reshape(PACKS, RESP_PACK).astype(jnp.int32)


def block_scale(stream_key, extent, shards, smallest, top_value):
    factor_of = 1.0
    for axis_at, parts in shards:
        heights = jax.random.uniform(jax.random.fold_in(jax.random.fold_in(stream_key, 6), axis_at), (parts,), jnp.float32, smallest / len(shards), top_value / len(shards))
        factor_of = factor_of * jnp.repeat(jnp.exp(heights), extent[axis_at] // parts).reshape((-1,) + (1,) * (len(extent) - 1 - axis_at))
    return factor_of


def normal_values(own_key, dims, deviation, bound, cuts=(), kind=jnp.bfloat16):
    array = jax.random.normal(own_key, dims, jnp.float32) * deviation
    if len(cuts) > 0:
        array = block_scale(own_key, dims, cuts, -0.22, 0.18) * array
    return jnp.clip(array, min=-bound, max=bound).astype(kind)


def setup_inputs(seed: int = 0) -> dict:
    seeds = jax.random.split(jax.random.key(seed), 10)
    queries = draw_queries(jax.random.fold_in(seeds[9], 71), 0)
    keys = draw_keys(jax.random.fold_in(seeds[9], 71), 0)
    values = normal_values(seeds[2], (PACKS, LENGTH, KVHEADS * HEAD_DIM), 1.0, 6.0, ((0, 8), (1, 96)))
    logp_grad = normal_values(seeds[3], (PACKS, LENGTH, QHEADS * HEAD_DIM), 1.0, 6.0, ((0, 8), (1, 96)))
    response_ids = draw_response_ids(jax.random.fold_in(seeds[9], 71), 0)
    sample_ids = draw_sample_ids(jax.random.fold_in(seeds[9], 71), 0)
    rewards = jnp.clip(1.0 * jax.random.uniform(seeds[6], (PACKS, RESP_PACK), jnp.float32) ** block_scale(seeds[6], (PACKS, RESP_PACK), ((0, 8),), -0.2, 0.2), 0.0, 1.0)
    new_logp = jnp.clip(-4.0 + 4.0 * jax.random.uniform(seeds[7], (PACKS, LENGTH), jnp.float32) ** block_scale(seeds[7], (PACKS, LENGTH), ((0, 8), (1, 96)), -0.2, 0.2), -4.0, 0.0)
    old_logp = jnp.clip(-4.0 + 4.0 * jax.random.uniform(seeds[8], (PACKS, LENGTH), jnp.float32) ** block_scale(seeds[8], (PACKS, LENGTH), ((0, 8), (1, 96)), -0.2, 0.2), -4.0, 0.0)
    return {"queries": queries, "keys": keys, "values": values, "logp_grad": logp_grad, "response_ids": response_ids, "sample_ids": sample_ids, "rewards": rewards, "new_logp": new_logp, "old_logp": old_logp}


def pack_attention(pieces):
    query_rows, key_rows, value_rows, grad_rows, start_rows = pieces
    block_rows = 4 * TOK_DEV
    back_rows = SPAN * TOK_DEV
    window_rows = block_rows + back_rows
    group_heads = QHEADS // KVHEADS
    score_scale = 1.0 / math.sqrt(HEAD_DIM)
    block_count = LENGTH // block_rows
    key_padded = jnp.pad(key_rows, ((back_rows, 0), (0, 0)))
    value_padded = jnp.pad(value_rows, ((back_rows, 0), (0, 0)))
    query_blocks = query_rows.reshape(block_count, block_rows, KVHEADS, group_heads, HEAD_DIM)
    grad_blocks = grad_rows.reshape(block_count, block_rows, KVHEADS, group_heads, HEAD_DIM)
    start_blocks = start_rows.reshape(block_count, block_rows)

    def block_step(accums, pieces_in):
        key_accum, value_accum = accums
        block_index, query_block, grad_block, start_block = pieces_in
        block_start = block_index * block_rows
        key_window = lax.dynamic_slice_in_dim(key_padded, block_start, window_rows, 0)
        value_window = lax.dynamic_slice_in_dim(value_padded, block_start, window_rows, 0)
        key_float = key_window.astype(jnp.float32).reshape(window_rows, KVHEADS, HEAD_DIM)
        value_float = value_window.astype(jnp.float32).reshape(window_rows, KVHEADS, HEAD_DIM)
        query_float = query_block.astype(jnp.float32)
        grad_float = lax.optimization_barrier(grad_block).astype(jnp.float32)
        query_pos = block_start + jnp.arange(block_rows, dtype=jnp.int32)
        key_pos = block_start - back_rows + jnp.arange(window_rows, dtype=jnp.int32)
        allowed = (key_pos[None, :] <= query_pos[:, None]) & (key_pos[None, :] >= start_block[:, None])
        scores = jnp.einsum('tghd,jgd->ghtj', query_float, key_float) * score_scale
        scores = jnp.where(allowed, scores, -jnp.inf)
        row_top = lax.optimization_barrier(jnp.max(scores, axis=-1, keepdims=True))
        powers = jnp.exp(scores - row_top)
        weights = powers / lax.optimization_barrier(jnp.sum(powers, axis=-1, keepdims=True))
        weights_bf = lax.optimization_barrier(weights.astype(jnp.bfloat16)).astype(jnp.float32)
        attended = jnp.einsum('ghtj,jgd->tghd', weights_bf, value_float)
        row_delta = jnp.transpose(lax.optimization_barrier(jnp.sum(grad_float * attended, axis=-1)), (1, 2, 0))
        dprob = jnp.einsum('tghd,jgd->ghtj', grad_float, value_float)
        dscore = weights * (dprob - row_delta[..., None])
        dscore = lax.optimization_barrier(dscore.astype(jnp.bfloat16)).astype(jnp.float32)
        query_part = (jnp.einsum('ghtj,jgd->tghd', dscore, key_float) * score_scale).astype(jnp.bfloat16)
        key_part = (jnp.einsum('ghtj,tghd->jgd', dscore, query_float) * score_scale).reshape(window_rows, KVHEADS * HEAD_DIM)
        value_part = jnp.einsum('ghtj,tghd->jgd', weights_bf, grad_float).reshape(window_rows, KVHEADS * HEAD_DIM)
        key_old = lax.dynamic_slice_in_dim(key_accum, block_start, window_rows, 0)
        value_old = lax.dynamic_slice_in_dim(value_accum, block_start, window_rows, 0)
        key_accum = lax.dynamic_update_slice_in_dim(key_accum, key_old + key_part, block_start, 0)
        value_accum = lax.dynamic_update_slice_in_dim(value_accum, value_old + value_part, block_start, 0)
        return ((key_accum, value_accum), query_part)
    zeros_init = jnp.zeros((LENGTH + back_rows, KVHEADS * HEAD_DIM), jnp.float32)
    indices = jnp.arange(block_count, dtype=jnp.int32)
    accums, query_parts = lax.scan(block_step, (zeros_init, zeros_init), (indices, query_blocks, grad_blocks, start_blocks))
    query_grad = query_parts.reshape(LENGTH, QHEADS * HEAD_DIM)
    return (query_grad, accums[0][back_rows:].astype(jnp.bfloat16), accums[1][back_rows:].astype(jnp.bfloat16))

def reference(queries, keys, values, logp_grad, response_ids, sample_ids, rewards, new_logp, old_logp):
    log_ratio = new_logp - old_logp

    def segment_total(row_vals, row_ids):
        return jax.ops.segment_sum(row_vals, row_ids, num_segments=RESP_PACK)
    seq_total = jax.vmap(segment_total)(log_ratio, response_ids)
    seq_length = jax.vmap(segment_total)(jnp.ones_like(log_ratio), response_ids)
    seq_ratio = jnp.exp(seq_total / seq_length)
    group_sum = jax.ops.segment_sum(rewards.reshape(-1), sample_ids.reshape(-1), num_segments=SAMPLES)
    advantage = rewards - group_sum[sample_ids] / GROUP
    seq_weight = -advantage * seq_ratio * MEAN_LEN / seq_length
    token_ratio = jnp.take_along_axis(seq_ratio, response_ids, axis=1)
    token_weight = jnp.take_along_axis(seq_weight, response_ids, axis=1)
    seq_start = jnp.cumsum(seq_length, axis=1) - seq_length
    token_start = jnp.take_along_axis(seq_start, response_ids, axis=1).astype(jnp.int32)
    out_grad = (token_weight[..., None] * logp_grad.astype(jnp.float32)).astype(jnp.bfloat16)
    query_grad, key_grad, value_grad = lax.map(pack_attention, (queries, keys, values, out_grad, token_start))
    return (query_grad, key_grad, value_grad, token_ratio, advantage)
```

```python
import math

import jax
import jax.numpy as jnp
from jax import lax
from jax.sharding import PartitionSpec as P

QHEADS = 32
KVHEADS = 4
HEAD_DIM = 128
SPAN = 3
GROUP = 8
MEAN_LEN = 256


def passed_along(array, axis, by):
    count = lax.axis_size(axis)
    pairs = [(i, i + by) for i in range(count) if 0 <= i + by < count]
    return lax.ppermute(array, axis, pairs)


def summed_over_dp(array):
    count = lax.axis_size("dp")
    step = 1
    while step < count:
        array = array + lax.ppermute(array, "dp", [(i, i ^ step) for i in range(count)])
        step *= 2
    return array


def shards(queries, keys, values, logp_grad, response_ids, sample_ids, rewards, new_logp, old_logp):
    highest = lax.Precision.HIGHEST
    tok_rows = queries.shape[1]
    ids = response_ids[0] + 1
    log_ratio = new_logp[0] - old_logp[0]
    own_keys = keys[0]
    own_values = values[0]
    arrived = [
        passed_along((own_keys, own_values), "ctx", distance) for distance in range(1, SPAN + 1)
    ]
    info = jnp.stack([ids.astype(jnp.float32), log_ratio])
    below = [passed_along(info, "ctx", distance) for distance in range(SPAN, 0, -1)]
    above = [passed_along(info, "ctx", -distance) for distance in range(1, SPAN + 1)]
    window = jnp.stack(below + [info] + above)
    window_ids = window[:, 0]
    window_logs = window[:, 1]
    first_id = info[0, 0]
    last_id = info[0, tok_rows - 1]
    of_first = window_ids == first_id
    of_last = window_ids == last_id
    first_count = jnp.sum(of_first.astype(jnp.float32))
    last_count = jnp.sum(of_last.astype(jnp.float32))
    first_total = jnp.sum(jnp.where(of_first, window_logs, 0.0))
    last_total = jnp.sum(jnp.where(of_last, window_logs, 0.0))
    resp_count = rewards.shape[1]
    group_count = lax.axis_size("dp") * resp_count // GROUP
    sample_hot = (
        sample_ids[0][:, None] == jnp.arange(group_count, dtype=jnp.int32)[None, :]
    ).astype(jnp.float32)
    own_rewards = rewards[0]
    group_sums = summed_over_dp(jnp.dot(own_rewards, sample_hot, precision=highest))
    advantage = own_rewards - jnp.dot(sample_hot, group_sums, precision=highest) / GROUP
    resp_range = jnp.arange(resp_count, dtype=jnp.int32) + 1
    first_adv = jnp.sum(jnp.where(resp_range == ids[0], advantage, 0.0))
    last_adv = jnp.sum(jnp.where(resp_range == ids[-1], advantage, 0.0))
    is_first = ids == ids[0]
    tok_total = jnp.where(is_first, first_total, last_total)
    tok_count = jnp.where(is_first, first_count, last_count)
    tok_ratio = jnp.exp(tok_total / tok_count)
    tok_adv = jnp.where(is_first, first_adv, last_adv)
    tok_weight = -tok_adv * tok_ratio * MEAN_LEN / tok_count
    ordered = arrived[::-1]
    key_window = jnp.concatenate([piece[0] for piece in ordered] + [own_keys], axis=0)
    value_window = jnp.concatenate([piece[1] for piece in ordered] + [own_values], axis=0)
    window_rows = key_window.shape[0]
    key_pos = jnp.arange(window_rows, dtype=jnp.int32) - SPAN * tok_rows
    query_pos = jnp.arange(tok_rows, dtype=jnp.int32)
    key_ids = window_ids[: SPAN + 1].reshape(window_rows)
    allowed = (key_pos[None, :] <= query_pos[:, None]) & (key_ids[None, :] == info[0][:, None])
    score_scale = 1.0 / math.sqrt(HEAD_DIM)
    group_heads = QHEADS // KVHEADS
    query_heads = queries[0].reshape(tok_rows, KVHEADS, group_heads, HEAD_DIM)
    grad_heads = logp_grad[0].reshape(tok_rows, KVHEADS, group_heads, HEAD_DIM)
    query_parts = []
    key_parts = []
    value_parts = []
    for kv_head in range(KVHEADS):
        query_group = query_heads[:, kv_head]
        grad_group = grad_heads[:, kv_head]
        key_group = key_window[:, kv_head * HEAD_DIM : (kv_head + 1) * HEAD_DIM]
        value_group = value_window[:, kv_head * HEAD_DIM : (kv_head + 1) * HEAD_DIM]
        scores = (
            jnp.einsum("thd,jd->htj", query_group, key_group, preferred_element_type=jnp.float32)
            * score_scale
        )
        scores = jnp.where(allowed[None], scores, -jnp.inf)
        row_top = jnp.max(scores, axis=-1, keepdims=True)
        powers = jnp.exp(scores - row_top)
        row_sum = jnp.sum(powers, axis=-1, keepdims=True)
        weights = powers / row_sum
        weights_bf = weights.astype(jnp.bfloat16)
        dprob = jnp.einsum(
            "thd,jd->htj", grad_group, value_group, preferred_element_type=jnp.float32
        )
        row_delta = jnp.sum(weights_bf.astype(jnp.float32) * dprob, axis=-1, keepdims=True)
        dscore = (weights * (dprob - row_delta)).astype(jnp.bfloat16)
        query_parts.append(
            jnp.einsum("htj,jd->thd", dscore, key_group, preferred_element_type=jnp.float32)
        )
        key_parts.append(
            jnp.einsum("htj,thd->jd", dscore, query_group, preferred_element_type=jnp.float32)
        )
        value_parts.append(
            jnp.einsum("htj,thd->jd", weights_bf, grad_group, preferred_element_type=jnp.float32)
        )
    scaled_weight = (tok_weight * score_scale)[:, None]
    query_grad = (
        jnp.stack(query_parts, axis=1).reshape(tok_rows, QHEADS * HEAD_DIM) * scaled_weight
    ).astype(jnp.bfloat16)
    key_full = jnp.concatenate(key_parts, axis=1)
    value_full = jnp.concatenate(value_parts, axis=1)

    def rows_for(matrix, distance):
        return matrix[(SPAN - distance) * tok_rows : (SPAN - distance + 1) * tok_rows]

    key_sum = rows_for(key_full, 0)
    value_sum = rows_for(value_full, 0)
    for distance in range(1, SPAN + 1):
        key_sum = key_sum + passed_along(
            rows_for(key_full, distance).astype(jnp.bfloat16), "ctx", -distance
        ).astype(jnp.float32)
        value_sum = value_sum + passed_along(
            rows_for(value_full, distance).astype(jnp.bfloat16), "ctx", -distance
        ).astype(jnp.float32)
    return (
        query_grad[None],
        (key_sum * scaled_weight).astype(jnp.bfloat16)[None],
        (value_sum * tok_weight[:, None]).astype(jnp.bfloat16)[None],
        tok_ratio[None],
        advantage[None],
    )


def solution(mesh):
    return jax.shard_map(
        shards,
        mesh=mesh,
        in_specs=(
            P("dp", "ctx", None),
            P("dp", "ctx", None),
            P("dp", "ctx", None),
            P("dp", "ctx", None),
            P("dp", "ctx"),
            P("dp", None),
            P("dp", None),
            P("dp", "ctx"),
            P("dp", "ctx"),
        ),
        out_specs=(
            P("dp", "ctx", None),
            P("dp", "ctx", None),
            P("dp", "ctx", None),
            P("dp", "ctx"),
            P("dp", None),
        ),
        check_vma=False,
    )
```

```python
import functools
import math

import jax
import jax.numpy as jnp
from jax import lax
from jax.experimental import pallas as pl
from jax.experimental.pallas import tpu as pltpu
from jax.sharding import PartitionSpec as P

QHEADS = 32
KVHEADS = 4
HEAD_DIM = 128
SPAN = 3
GROUP = 8
MEAN_LEN = 256
GROUP_HEADS = QHEADS // KVHEADS
INFO_ROWS = 16
CORES = 2
CHUNKS = 2
CHUNK_HEADS = KVHEADS // CHUNKS
PAIR = 2 * HEAD_DIM
SCORE_SCALE = 1.0 / math.sqrt(HEAD_DIM)
HIDDEN = -1e30


def passed_along(array, axis, by, around=False):
    count = lax.axis_size(axis)
    pairs = [(i, (i + by) % count) for i in range(count) if around or 0 <= i + by < count]
    return lax.ppermute(array, axis, pairs)


def from_other_core(array):
    return lax.ppermute(array, "dp", [(i, i ^ CORES - 1) for i in range(lax.axis_size("dp"))])


def turn(at, chips):
    return 1 + at % (chips - 1)


def from_turned(array):
    ranks, count = lax.axis_size("dp"), lax.axis_size("ctx")
    chips = ranks // CORES
    if chips == 1:
        return jnp.zeros_like(array)
    pairs = [
        ((rank + turn(at, chips) * CORES) % ranks * count + at, rank * count + at)
        for rank in range(ranks)
        for at in range(count)
    ]
    return lax.ppermute(array, ("dp", "ctx"), pairs)


def forward(packed, sums):
    came = []
    first, second = packed
    turned = None
    for hop in range(SPAN):
        first = passed_along(first, "ctx", 1)
        second = passed_along(second, "ctx", 1)
        if hop == 0:
            sums = sums + from_other_core(sums)
            first, sums = lax.optimization_barrier((first, sums))
        if hop == 1:
            turned = from_turned(sums)
            first, turned = lax.optimization_barrier((first, turned))
        came.append([first, second])
    return came, sums, turned


def eye(size):
    rows = lax.broadcasted_iota(jnp.int32, (size, size), 0)
    return rows == lax.broadcasted_iota(jnp.int32, (size, size), 1)


def sample_hot(sample_ids, groups):
    shape = (groups, sample_ids.shape[1])
    return lax.broadcasted_iota(jnp.int32, shape, 0) == sample_ids


def with_lines(info, first, line):
    high = line.astype(jnp.bfloat16).astype(jnp.float32)
    middle = (line - high).astype(jnp.bfloat16).astype(jnp.float32)
    at = lax.broadcasted_iota(jnp.int32, info.shape, 0)
    for k, part in enumerate((high, middle, line - high - middle)):
        info = jnp.where(at == first + k, part, info)
    return info


def line_of(block, first):
    return block[first : first + 1] + block[first + 1 : first + 2] + block[first + 2 : first + 3]


def pack_body(keys, values, ids, new_logp, old_logp, sample_ids, rewards, *outs):
    *packed, sums = outs
    rows = keys.shape[0]
    log_ratio = new_logp[...] - old_logp[...]
    at = lax.broadcasted_iota(jnp.int32, (INFO_ROWS, rows), 0)
    info = jnp.where(at == 0, (ids[...] + 1).astype(jnp.float32), 0.0)
    info = with_lines(info, 1, log_ratio).astype(jnp.bfloat16)
    for head in range(KVHEADS):
        columns = slice(head * HEAD_DIM, (head + 1) * HEAD_DIM)
        out = packed[head // CHUNK_HEADS]
        at = 2 * (head % CHUNK_HEADS) * rows
        out[at : at + rows, :] = keys[:, columns]
        out[at + rows : at + 2 * rows, :] = values[:, columns]
    packed[0][2 * CHUNK_HEADS * rows :, :] = info
    groups = sums.shape[1]
    hot = sample_hot(sample_ids[...], groups)
    column = jnp.sum(jnp.where(hot, rewards[...], 0.0), axis=1, keepdims=True)
    sums[...] = jnp.sum(jnp.where(eye(groups), column, 0.0), axis=0, keepdims=True)


def over_lanes(ref):
    return ref[0:1, :].astype(jnp.float32)


def advantage_of(sums, turned, others, sample_ids, rewards):
    chips = lax.axis_size("dp") // CORES
    chip = lax.axis_index("dp") // CORES
    at = lax.axis_index("ctx")
    held = [(chip, sums[...])]
    if chips > 1:
        lines = [turned[...]] + [line_of(block, 4) for block in others[: chips - 2]]
        held += [((chip + turn(at + k, chips)) % chips, line) for k, line in enumerate(lines)]
    total = jnp.zeros_like(sums)
    for wanted in range(chips):
        for source, line in held:
            total = total + jnp.where(source == wanted, line, 0.0)
    hot = sample_hot(sample_ids[...], sums.shape[1])
    column = jnp.sum(jnp.where(eye(sums.shape[1]), total, 0.0), axis=1, keepdims=True)
    return rewards[...] - jnp.sum(jnp.where(hot, column, 0.0), axis=0, keepdims=True) / GROUP


def attention_body(chunk, q_ref, g_ref, own_info, own, came1, came2, came3, *rest):
    rows = q_ref.shape[0]
    step = pl.program_id(0)
    infos = [ref.at[2 * CHUNK_HEADS * rows :, :] for ref in (came1, came2, came3)]
    came = (came1, came2, came3)
    if chunk:
        came, rest = rest[:3], rest[3:]
    else:
        turned, rest = rest[0], rest[1:]
    dq_ref, sum0, sum1, sum2, sum3 = rest
    out_rows = pl.ds(pl.multiple_of(step * 2 * rows, 2 * rows), 2 * rows)
    pairs = [own[...]] + [ref[out_rows, :] for ref in came]
    own_ids = over_lanes(own_info)
    first = own_ids[:, 0:1]

    def count(ids):
        return jnp.sum((ids == first).astype(jnp.float32), axis=1, keepdims=True)

    head_count = count(own_ids).astype(jnp.int32)
    below = sum(count(over_lanes(ref)) for ref in infos).astype(jnp.int32)
    key_at = lax.broadcasted_iota(jnp.int32, (rows, rows), 0)
    query_at = lax.broadcasted_iota(jnp.int32, (rows, rows), 1)
    near = key_at <= query_at
    start = jnp.where(query_at < head_count, -below, head_count)

    def bias(at):
        return jnp.where(at >= start, 0.0, HIDDEN)

    hidden = jnp.concatenate(
        [
            bias(jnp.where(near, key_at, key_at - SPAN * rows)),
            bias(key_at - rows),
            bias(key_at - 2 * rows),
        ],
        axis=0,
    )
    pairs = [pairs[3], pairs[0], pairs[1], pairs[2]]
    key_rows = jnp.concatenate([pair[:rows] for pair in pairs], axis=0)
    value_rows = jnp.concatenate([pair[rows:] for pair in pairs], axis=0)

    def stacked(ref):
        return jnp.concatenate(
            [ref[:, h * HEAD_DIM : (h + 1) * HEAD_DIM] for h in range(GROUP_HEADS)], axis=0
        )

    def merged(tall):
        return jnp.concatenate(
            [jnp.where(near, tall[rows : 2 * rows], tall[:rows]), tall[2 * rows :]], axis=0
        )

    def parted(short):
        blank = jnp.zeros((rows, rows), jnp.bfloat16)
        return jnp.concatenate(
            [
                jnp.where(near, blank, short[:rows]),
                jnp.where(near, short[:rows], blank),
                short[rows:],
            ],
            axis=0,
        )

    query_rows = stacked(q_ref)
    grad_rows = stacked(g_ref)
    minor = (((1,), (1,)), ((), ()))
    scores = lax.dot_general(key_rows, query_rows, minor, preferred_element_type=jnp.float32)
    dprob = lax.dot_general(value_rows, grad_rows, minor, preferred_element_type=jnp.float32)
    to_power = SCORE_SCALE * math.log2(math.e)
    weight_parts = []
    dscore_parts = []
    for h in range(GROUP_HEADS):
        lanes = slice(h * rows, (h + 1) * rows)
        part = merged(scores[:, lanes]) + hidden
        top = jnp.max(part, axis=0, keepdims=True)
        powers = jnp.exp2((part - top) * to_power)
        weights = powers * (1.0 / jnp.sum(powers, axis=0, keepdims=True))
        grads = merged(dprob[:, lanes])
        delta = jnp.sum(weights * grads, axis=0, keepdims=True)
        weight_parts.append(parted(weights.astype(jnp.bfloat16)))
        dscore_parts.append(parted((weights * (grads - delta)).astype(jnp.bfloat16)))
    weights_bf = jnp.concatenate(weight_parts, axis=1)
    dscore = jnp.concatenate(dscore_parts, axis=1)
    value_part = jnp.dot(weights_bf, grad_rows, preferred_element_type=jnp.float32)
    key_part = jnp.dot(dscore, query_rows, preferred_element_type=jnp.float32)
    query_part = jnp.dot(key_rows.T, dscore, preferred_element_type=jnp.float32)
    for h in range(GROUP_HEADS):
        lanes = slice(h * rows, (h + 1) * rows)
        dq_ref[:, h * HEAD_DIM : (h + 1) * HEAD_DIM] = query_part[:, lanes].T.astype(jnp.bfloat16)
    for at, out in enumerate((sum3, sum0, sum1, sum2)):
        lines = slice(at * rows, (at + 1) * rows)
        at_rows = slice(None) if out is sum0 else out_rows
        out[at_rows, :] = jnp.concatenate(
            [key_part[lines].astype(out.dtype), value_part[lines].astype(out.dtype)], axis=0
        )
    if not chunk:
        base = 2 * CHUNK_HEADS * rows
        sum3[base:, :] = with_lines(own_info[...].astype(jnp.float32), 4, turned[...]).astype(
            sum3.dtype
        )
        for out in (sum2, sum1):
            out[base:, :] = jnp.zeros((INFO_ROWS, HEAD_DIM), out.dtype)


def weights_of(own_info, blocks, advantage):
    rows = own_info.shape[1]
    own_ids = over_lanes(own_info)
    first = own_ids[:, 0:1]
    last = own_ids[:, rows - 1 : rows]
    resp_at = (lax.broadcasted_iota(jnp.int32, advantage.shape, 1) + 1).astype(jnp.float32)
    logs = [line_of(block, 1) for block in blocks]

    def of_response(wanted):
        totals = jnp.zeros((1, rows), jnp.float32)
        counts = jnp.zeros((1, rows), jnp.float32)
        for block, log in zip(blocks, logs):
            same = block[0:1] == wanted
            totals = totals + jnp.where(same, log, 0.0)
            counts = counts + jnp.where(same, 1.0, 0.0)
        total = jnp.sum(totals, axis=1, keepdims=True)
        length = jnp.sum(counts, axis=1, keepdims=True)
        gain = jnp.sum(jnp.where(resp_at == wanted, advantage, 0.0), axis=1, keepdims=True)
        ratio = jnp.exp(total / length)
        return ratio, -gain * ratio * MEAN_LEN / length

    first_ratio, first_weight = of_response(first)
    last_ratio, last_weight = of_response(last)
    head_count = jnp.sum((own_ids == first).astype(jnp.float32), axis=1, keepdims=True)
    row_at = lax.broadcasted_iota(jnp.int32, (rows, 1), 0)
    weight = jnp.where(row_at < head_count.astype(jnp.int32), first_weight, last_weight)
    return jnp.where(own_ids == first, first_ratio, last_ratio), weight


def write_kv(weight, sum0, came, dk_out, dv_out):
    rows = dk_out.shape[0]
    for head in range(CHUNK_HEADS):
        columns = slice(head * HEAD_DIM, (head + 1) * HEAD_DIM)
        for at, out, scale in ((0, dk_out, weight * SCORE_SCALE), (1, dv_out, weight)):
            lines = slice((2 * head + at) * rows, (2 * head + at + 1) * rows)
            whole = sum0[lines, :] + came[lines, :].astype(jnp.float32)
            out[:, columns] = (whole * scale).astype(jnp.bfloat16)


def on_chip(array):
    return pltpu.with_memory_space_constraint(array, pltpu.VMEM)


def final_body(own_info, *refs):
    came, back = refs[:3], refs[3:6]
    sums, turned, sample_ids, rewards, sum0 = refs[6:11]
    parts = refs[11:-6]
    dq_out, dk_out, dv_out, ratio_out, weight_out, advantage_out = refs[-6:]
    base = sum0.shape[0]
    blocks = [own_info[...].astype(jnp.float32)]
    blocks += [ref[base:, :].astype(jnp.float32) for ref in (*came, *back)]
    advantage = advantage_of(sums, turned, blocks[SPAN + 1 :], sample_ids, rewards)
    advantage_out[...] = advantage
    ratio_out[...], weight = weights_of(own_info, blocks, advantage)
    weight_out[...] = jnp.broadcast_to(weight, weight_out.shape)
    scaled = weight * SCORE_SCALE
    left = 0
    for part in parts:
        right = left + part.shape[1]
        dq_out[:, left:right] = (part[...].astype(jnp.float32) * scaled).astype(jnp.bfloat16)
        left = right
    write_kv(weight, sum0, back[2], dk_out, dv_out)


def rest_body(weight, sum0, came, dk_in, dv_in, dk_out, dv_out):
    del dk_in, dv_in
    write_kv(weight[:, 0:1], sum0, came, dk_out, dv_out)


def shards(queries, keys, values, logp_grad, response_ids, sample_ids, rewards, new_logp, old_logp):
    rows = queries.shape[1]
    resp_count = rewards.shape[1]
    group_width = GROUP_HEADS * HEAD_DIM
    kv_width = CHUNK_HEADS * HEAD_DIM
    bf = jnp.bfloat16
    height = 2 * CHUNK_HEADS * rows
    talls = [height if c else height + INFO_ROWS for c in range(CHUNKS)]
    *packed, sums = pl.pallas_call(
        pack_body,
        out_shape=[
            *[jax.ShapeDtypeStruct((tall, HEAD_DIM), bf) for tall in talls],
            jax.ShapeDtypeStruct((1, HEAD_DIM), jnp.float32),
        ],
        name="pack",
    )(keys[0], values[0], response_ids, new_logp, old_logp, sample_ids, rewards)
    came, sums, turned = forward(packed, sums)
    came = [[on_chip(piece) for piece in pieces] for pieces in came]
    info_spec = pl.BlockSpec((INFO_ROWS, HEAD_DIM), lambda g: (height // INFO_ROWS, 0))
    chip_spec = pl.BlockSpec(memory_space=pltpu.VMEM)
    line_spec = pl.BlockSpec((1, HEAD_DIM), lambda g: (0, 0))
    resp = pl.BlockSpec((1, resp_count), lambda g: (0, 0))
    parts = []
    for c in range(CHUNKS):
        head_spec = pl.BlockSpec((rows, group_width), lambda g, c=c: (0, g + c * CHUNK_HEADS))
        own_spec = pl.BlockSpec((2 * rows, HEAD_DIM), lambda g: (g, 0))
        more_specs, more = [line_spec], [turned]
        if c:
            more_specs, more = [chip_spec] * 3, [pieces[c] for pieces in came]
        parts.append(
            pl.pallas_call(
                functools.partial(attention_body, c),
                grid=(CHUNK_HEADS,),
                in_specs=[head_spec, head_spec, info_spec, own_spec]
                + [chip_spec] * 3
                + more_specs,
                out_specs=[
                    pl.BlockSpec((rows, group_width), lambda g: (0, g)),
                    pl.BlockSpec((2 * rows, HEAD_DIM), lambda g: (g, 0)),
                ]
                + [chip_spec] * 3,
                out_shape=[
                    jax.ShapeDtypeStruct((rows, CHUNK_HEADS * group_width), bf),
                    jax.ShapeDtypeStruct((height, HEAD_DIM), jnp.float32),
                ]
                + [pltpu.VMEM((talls[c], HEAD_DIM), bf)] * 3,
                name=f"attention{c}",
            )(queries[0], logp_grad[0], packed[0], packed[c], *[pieces[0] for pieces in came], *more)
        )
    back = []
    at = [part[4] for part in parts]
    for hop in range(SPAN):
        at = [passed_along(piece, "ctx", -1, around=c == 0) for c, piece in enumerate(at)]
        back.append(on_chip(at[0]))
        if hop < SPAN - 1:
            at = [piece + part[3 - hop] for piece, part in zip(at, parts)]

    def whole(shape, at=(0, 0)):
        return pl.BlockSpec(shape, lambda g: at)

    query_grad, key_grad, value_grad, token_ratio, weight, advantage = pl.pallas_call(
        final_body,
        grid=(1,),
        in_specs=[info_spec]
        + [chip_spec] * 6
        + [line_spec, line_spec, resp, resp, whole((height, HEAD_DIM))]
        + [whole((rows, CHUNK_HEADS * group_width))] * CHUNKS,
        out_specs=[
            whole((rows, queries.shape[2])),
            whole((rows, kv_width)),
            whole((rows, kv_width)),
            whole((1, rows)),
            whole((rows, HEAD_DIM)),
            resp,
        ],
        out_shape=[
            jax.ShapeDtypeStruct((rows, queries.shape[2]), bf),
            jax.ShapeDtypeStruct((rows, keys.shape[2]), bf),
            jax.ShapeDtypeStruct((rows, keys.shape[2]), bf),
            jax.ShapeDtypeStruct((1, rows), jnp.float32),
            jax.ShapeDtypeStruct((rows, HEAD_DIM), jnp.float32),
            jax.ShapeDtypeStruct((1, resp_count), jnp.float32),
        ],
        name="final",
    )(packed[0], *[pieces[0] for pieces in came], *back, sums, turned, sample_ids,
      rewards, parts[0][1], *[part[0] for part in parts])
    kv_spec = whole((rows, kv_width), (0, 1))
    any_spec = pl.BlockSpec(memory_space=pl.ANY)
    key_grad, value_grad = pl.pallas_call(
        rest_body,
        grid=(1,),
        in_specs=[
            whole((rows, HEAD_DIM)),
            whole((height, HEAD_DIM)),
            chip_spec,
            any_spec,
            any_spec,
        ],
        out_specs=[kv_spec, kv_spec],
        out_shape=[jax.ShapeDtypeStruct((rows, keys.shape[2]), bf)] * 2,
        input_output_aliases={3: 0, 4: 1},
        name="rest",
    )(weight, parts[1][1], on_chip(at[1]), key_grad, value_grad)
    return (query_grad[None], key_grad[None], value_grad[None], token_ratio, advantage)


def solution(mesh):
    return jax.shard_map(
        shards,
        mesh=mesh,
        in_specs=(
            P("dp", "ctx", None),
            P("dp", "ctx", None),
            P("dp", "ctx", None),
            P("dp", "ctx", None),
            P("dp", "ctx"),
            P("dp", None),
            P("dp", None),
            P("dp", "ctx"),
            P("dp", "ctx"),
        ),
        out_specs=(
            P("dp", "ctx", None),
            P("dp", "ctx", None),
            P("dp", "ctx", None),
            P("dp", "ctx"),
            P("dp", None),
        ),
        check_vma=False,
    )
```
